32 devices in a mesh: section: 2 (over core), ctx: 4 (over z), fsdp: 4 (over y, x).
Axes of the slice: x: 2, y: 2, z: 4, core: 2. Of those that a mesh axis runs over, the one named last changes fastest.
Arguments:
- block_input: bfloat16 [24, 1024, 768], P('fsdp', 'ctx'), may hold values from -6 to 6
- positions: int32 [24, 1024], P('fsdp'), may hold values from 0 to 1023, each once within a row
- cotangent: bfloat16 [24, 1024, 768], P('fsdp', 'ctx'), may hold values from -6 to 6
- w_qkv: bfloat16 [2, 768, 2304], P('section', 'fsdp'), may hold values from -0.21875 to 0.21875
- w_proj: bfloat16 [2, 768, 768], P('section', 'fsdp'), may hold values from -1.25 to 1.25
- w_fc: bfloat16 [2, 768, 3072], P('section', 'fsdp'), may hold values from -0.21875 to 0.21875
- w_out: bfloat16 [2, 3072, 768], P('section', 'fsdp'), may hold values from -0.109375 to 0.109375
- ln_gain: bfloat16 [2, 2, 768], P('section', None, 'fsdp'), may hold values from 0.099609375 to 1.8984375
- ln_bias: bfloat16 [2, 2, 768], P('section', None, 'fsdp'), may hold values from -1.75 to 1.75
- attn_bias: bfloat16 [2, 2, 768], P('section', None, 'fsdp'), may hold values from -3 to 3
- out_bias: bfloat16 [2, 2, 768], P('section', None, 'fsdp'), may hold values from -1.75 to 1.75
- fc_bias: bfloat16 [2, 3072], P('section', 'fsdp'), may hold values from -3 to 3
Outputs:
- section_out: bfloat16 [2, 24, 1024, 768], P('section', 'fsdp', 'ctx')
- section_in_grad: bfloat16 [2, 24, 1024, 768], P('section', 'fsdp', 'ctx')
- grad_w_qkv: float32 [2, 768, 2304], P('section', 'fsdp')
- grad_w_proj: float32 [2, 768, 768], P('section', 'fsdp')
- grad_w_fc: float32 [2, 768, 3072], P('section', 'fsdp')
- grad_w_out: float32 [2, 3072, 768], P('section', 'fsdp')
- grad_ln_gain: float32 [2, 2, 768], P('section', None, 'fsdp')
- grad_ln_bias: float32 [2, 2, 768], P('section', None, 'fsdp')
- grad_attn_bias: float32 [2, 2, 768], P('section', None, 'fsdp')
- grad_out_bias: float32 [2, 2, 768], P('section', None, 'fsdp')
- grad_fc_bias: float32 [2, 3072], P('section', 'fsdp')
The draws below stay inside these ranges and needn't reach their ends.
Inputs may be any that keep to these rules, and one draw needn't show every extreme that they name: `positions`: each row is a permutation of the places 0 to 1023 of one sequence.
All inputs are finite; a program needn't handle non-finite values.
Results may differ from the reference program's by a relative error of at most 0.034.
Values may be sent and summed in bfloat16 or wider, within the bound.
A program may use at most 320 MiB of HBM per device.

```python
import math
import jax
import jax.numpy as jnp
from jax import lax

D = 768
H = 12
HD = 64
FF = 3072
SEQ = 1024
SEQS = 24


def levels(own_key, dims, shards, smallest, largest):
    def one(dim, shards_of):
        draws = jax.random.uniform(jax.random.fold_in(jax.random.fold_in(own_key, 6), dim), (shards_of,), jnp.float32, smallest / len(shards), largest / len(shards))
        return jnp.repeat(jnp.exp(draws), dims[dim] // shards_of).reshape((-1,) + (1,) * (len(dims) - dim - 1))

    level = one(*shards[0])
    for cut in shards[1:]:
        level = level * one(*cut)
    return level


def scatter_about(own_key, shape, scale, bound, pieces=(), kind=jnp.bfloat16):
    array = jax.random.normal(own_key, shape, jnp.float32) * scale
    if len(pieces) > 0:
        array = levels(own_key, shape, pieces, -0.22, 0.18) * array
    return jnp.clip(array, min=-bound, max=bound).astype(kind)


def setup_inputs(seed: int = 0) -> dict:
    streams_of = jax.random.split(jax.random.key(seed), 13)
    return {
        "block_input": scatter_about(streams_of[0], (SEQS, SEQ, D), 1.0, 6.0, ((0, 4), (1, 4))),
        "positions": jax.vmap(lambda own: jax.random.permutation(own, SEQ))(jax.random.split(streams_of[1], SEQS)).reshape((SEQS, SEQ)).astype(jnp.int32),
        "cotangent": scatter_about(streams_of[2], (SEQS, SEQ, D), 1.0, 6.0, ((0, 4), (1, 4))),
        "w_qkv": scatter_about(streams_of[3], (2, D, 3 * D), D ** -0.5, 0.21875, ((0, 2), (1, 4))),
        "w_proj": scatter_about(streams_of[4], (2, D, D), (D // 32) ** -0.5, 1.25, ((0, 2), (1, 4))),
        "w_fc": scatter_about(streams_of[5], (2, D, FF), D ** -0.5, 0.21875, ((0, 2), (1, 4))),
        "w_out": scatter_about(streams_of[6], (2, FF, D), FF ** -0.5, 0.109375, ((0, 2), (1, 4))),
        "ln_gain": jnp.clip(1.0 + 0.18 * jax.random.normal(streams_of[7], (2, 2, D), jnp.float32), 0.099609375, 1.8984375).astype(jnp.bfloat16),
        "ln_bias": scatter_about(streams_of[8], (2, 2, D), 0.3, 1.75, ((0, 2), (2, 4))),
        "attn_bias": scatter_about(streams_of[9], (2, 2, D), 0.5, 3.0, ((0, 2), (2, 4))),
        "out_bias": scatter_about(streams_of[10], (2, 2, D), 0.3, 1.75, ((0, 2), (2, 4))),
        "fc_bias": scatter_about(streams_of[11], (2, FF), 0.5, 3.0, ((0, 2), (1, 4))),
    }


@jax.custom_vjp
def low(v):
    return lax.optimization_barrier(v.astype(jnp.bfloat16)).astype(jnp.float32)

@jax.custom_vjp
def low_back(v):
    return v

def low_keep(v):
    return (low(v), None)

def low_pass(kept, grad):
    return (grad,)

def back_keep(v):
    return (v, None)

def back_low(kept, grad):
    return (low(grad),)
low.defvjp(low_keep, low_pass)
low_back.defvjp(back_keep, back_low)

def layer_norm(hidden, gain, offset):
    center = hidden - lax.optimization_barrier(jnp.mean(hidden, axis=-1, keepdims=True))
    spread = lax.optimization_barrier(jnp.mean(center * center, axis=-1, keepdims=True))
    return center * lax.rsqrt(spread + 1e-05) * gain + offset

def matmul(rows, matrix):
    return jnp.einsum('nsd,de->nse', rows, matrix, precision=lax.Precision.HIGHEST)

def attend_single(item):
    queries, key_rows, value_rows, places = item
    query_heads = queries.reshape(SEQ, H, HD)
    key_heads = key_rows.reshape(SEQ, H, HD)
    value_heads = value_rows.reshape(SEQ, H, HD)
    scores = low_back(jnp.einsum('qhd,khd->hqk', query_heads, key_heads, precision=lax.Precision.HIGHEST) * HD ** (-0.5))
    allowed = places[:, None] >= places[None, :]
    scores = jnp.where(allowed[None], scores, -1e+30)
    probs = jax.nn.softmax(scores, axis=-1)
    mixed = jnp.einsum('hqk,khd->qhd', low(probs), value_heads, precision=lax.Precision.HIGHEST)
    return mixed.reshape(SEQ, D)

def layer(params, hidden, places):
    w_qkv, w_proj, w_fc, w_out, gains, offsets, attn_bias, out_bias, fc_bias = params
    normed = low(layer_norm(hidden, gains[0], offsets[0]))
    project = matmul(normed, w_qkv)
    queries = low_back(low(project[..., :D] + attn_bias[0]))
    key_rows = low_back(low(project[..., D:2 * D]))
    value_rows = low_back(low(project[..., 2 * D:] + attn_bias[1]))
    mixed = lax.map(jax.checkpoint(attend_single), (queries, key_rows, value_rows, places))
    mixed = low_back(low(mixed))
    branch = low_back(matmul(mixed, w_proj) + out_bias[0])
    after = hidden + branch
    normed_two = low(layer_norm(after, gains[1], offsets[1]))
    inner = low_back(matmul(normed_two, w_fc) + fc_bias)
    active = low(jax.nn.gelu(inner, approximate=True))
    return after + matmul(active, w_out) + out_bias[1]

def reference(block_input, positions, cotangent, w_qkv, w_proj, w_fc, w_out, ln_gain, ln_bias, attn_bias, out_bias, fc_bias):
    stacked = tuple((arr.astype(jnp.float32) for arr in (w_qkv, w_proj, w_fc, w_out, ln_gain, ln_bias, attn_bias, out_bias, fc_bias)))
    first = tuple((arr[0] for arr in stacked))
    second = tuple((arr[1] for arr in stacked))
    group = math.gcd(SEQS, 4)
    count = SEQS // group
    inputs = block_input.astype(jnp.float32).reshape(count, group, SEQ, D)
    places_all = positions.reshape(count, group, SEQ)
    cotans = cotangent.astype(jnp.float32).reshape(count, group, SEQ, D)

    def one_group(totals, item):
        hidden, places, cotan = item

        def run(params, rows):
            return layer(params, rows, places)
        middle_raw, pull_first = jax.vjp(run, first, hidden)
        middle = low(middle_raw)
        final, pull_second = jax.vjp(run, second, middle)
        grads_second, grad_middle = pull_second(cotan)
        grad_middle = low(grad_middle)
        grads_first, grad_hidden = pull_first(grad_middle)
        totals = tuple((total + jnp.stack([one, two]) for total, one, two in zip(totals, grads_first, grads_second)))
        return (totals, (middle, final, grad_hidden, grad_middle))
    zeros_init = tuple((jnp.zeros(arr.shape, jnp.float32) for arr in stacked))
    totals, (middle, final, grad_hidden, grad_middle) = lax.scan(one_group, zeros_init, (inputs, places_all, cotans))
    section_out = jnp.stack([middle.reshape(SEQS, SEQ, D), final.reshape(SEQS, SEQ, D)]).astype(jnp.bfloat16)
    section_in_grad = jnp.stack([grad_hidden.reshape(SEQS, SEQ, D), grad_middle.reshape(SEQS, SEQ, D)]).astype(jnp.bfloat16)
    return (section_out, section_in_grad, totals[0], totals[1], totals[2], totals[3], totals[4], totals[5], totals[6], totals[7], totals[8])
```

```python
import functools

import jax
import jax.numpy as jnp
from jax import lax
from jax.experimental import pallas as pl
from jax.experimental.pallas import tpu as pltpu
from jax.sharding import PartitionSpec as P

H = 12
HD = 64
PAIR = 2 * HD
SCALE = HD**-0.5

masked_score = -1e30
norm_eps = 1e-05
f32 = jnp.float32
bf16 = jnp.bfloat16


def layer_norm(hidden, gain, offset):
    center = hidden - jnp.mean(hidden, axis=-1, keepdims=True)
    spread = jnp.mean(center * center, axis=-1, keepdims=True)
    return center * lax.rsqrt(spread + norm_eps) * gain + offset


def gelu_tanh(inputs):
    return jax.nn.gelu(inputs, approximate=True)


def mm(left, right):
    return lax.dot_general(left, right, (((1,), (0,)), ((), ())), preferred_element_type=f32)


def mm_nt(left, right):
    return lax.dot_general(left, right, (((1,), (1,)), ((), ())), preferred_element_type=f32)


def mm_tn(left, right):
    return lax.dot_general(left, right, (((0,), (0,)), ((), ())), preferred_element_type=f32)


def masked_scores(keys, queries, start, block):
    scores = mm_nt(keys, queries)
    down = lax.broadcasted_iota(jnp.int32, (block, block), 0)
    across = lax.broadcasted_iota(jnp.int32, (block, block), 1)
    corner = jnp.where(across >= down, scores[start:], masked_score)
    if start == 0:
        return corner
    return jnp.concatenate([scores[:start], corner], axis=0)


def attend_kernel(block, q_ref, k_ref, v_ref, o_ref, log_ref):
    length = q_ref.shape[0]
    for head in range(2):
        cols = slice(head * HD, (head + 1) * HD)
        for start in range(0, length, block):
            end = start + block
            queries = (q_ref[start:end, cols].astype(f32) * SCALE).astype(bf16)
            scores = masked_scores(k_ref[:end, cols], queries, start, block)
            top = jnp.max(scores, axis=0, keepdims=True)
            weights = jnp.exp(scores - top)
            total = jnp.sum(weights, axis=0, keepdims=True)
            mixed = mm_tn(v_ref[:end, cols], weights.astype(bf16)) / total
            o_ref[start:end, cols] = mixed.T.astype(bf16)
            log_ref[0, 0, head : head + 1, start:end] = top + jnp.log(total)


def attend_back_kernel(
    block, q_ref, k_ref, v_ref, do_ref, o_ref, log_ref, dq_ref, dk_ref, dv_ref, dk_sum, dv_sum
):
    length = q_ref.shape[0]
    for head in range(2):
        cols = slice(head * HD, (head + 1) * HD)
        for start in range(length - block, -1, -block):
            end = start + block
            queries = (q_ref[start:end, cols].astype(f32) * SCALE).astype(bf16)
            grads = do_ref[start:end, cols]
            product = grads.astype(f32) * o_ref[start:end, cols].astype(f32)
            delta = jnp.sum(product.T, axis=0, keepdims=True)
            keys = k_ref[:end, cols]
            scores = masked_scores(keys, queries, start, block)
            probs = jnp.exp(scores - log_ref[0, 0, head : head + 1, start:end])
            grad_probs = mm_nt(v_ref[:end, cols], grads)
            grad_scores = (probs * (grad_probs - delta)).astype(bf16)
            dv = mm(probs.astype(bf16), grads)
            dk = mm(grad_scores, queries)
            if end == length:
                dv_sum[:end, cols] = dv
                dk_sum[:end, cols] = dk
            else:
                dv_sum[:end, cols] += dv
                dk_sum[:end, cols] += dk
            dq = mm_tn(keys, grad_scores) * SCALE
            dq_ref[start:end, cols] = dq.T.astype(bf16)
    dk_ref[...] = dk_sum[...].astype(bf16)
    dv_ref[...] = dv_sum[...].astype(bf16)


def query_block(length):
    return 256 if length % 256 == 0 else length


def head_spec(length, offset):
    return pl.BlockSpec((length, PAIR), lambda b, h: (b, offset + h))


def log_spec(length):
    return pl.BlockSpec((1, 1, 2, length), lambda b, h: (b, h, 0, 0))


def attend_forward(project, length):
    rows = project.shape[0]
    count = rows // length
    pairs = H // 2
    return pl.pallas_call(
        functools.partial(attend_kernel, query_block(length)),
        grid=(count, pairs),
        in_specs=[head_spec(length, 0), head_spec(length, pairs), head_spec(length, 2 * pairs)],
        out_specs=[head_spec(length, 0), log_spec(length)],
        out_shape=[
            jax.ShapeDtypeStruct((rows, H * HD), bf16),
            jax.ShapeDtypeStruct((count, pairs, 2, length), f32),
        ],
        compiler_params=pltpu.CompilerParams(vmem_limit_bytes=40 * 1024 * 1024),
        cost_estimate=pl.CostEstimate(
            flops=8 * rows * length * H * HD,
            bytes_accessed=8 * rows * H * HD,
            transcendentals=rows * length * H // 2,
        ),
    )(project, project, project)


def attend_back(project, grad_mixed, mixed, log_total, length):
    rows = project.shape[0]
    count = rows // length
    pairs = H // 2
    return pl.pallas_call(
        functools.partial(attend_back_kernel, query_block(length)),
        grid=(count, pairs),
        in_specs=[
            head_spec(length, 0),
            head_spec(length, pairs),
            head_spec(length, 2 * pairs),
            head_spec(length, 0),
            head_spec(length, 0),
            log_spec(length),
        ],
        out_specs=[head_spec(length, 0)] * 3,
        out_shape=[jax.ShapeDtypeStruct((rows, H * HD), bf16)] * 3,
        scratch_shapes=[pltpu.VMEM((length, PAIR), f32)] * 2,
        compiler_params=pltpu.CompilerParams(vmem_limit_bytes=40 * 1024 * 1024),
        cost_estimate=pl.CostEstimate(
            flops=20 * rows * length * H * HD,
            bytes_accessed=16 * rows * H * HD,
            transcendentals=rows * length * H // 2,
        ),
    )(project, project, project, grad_mixed, mixed, log_total)


def layer_forward(weights, smalls, layer_in, length):
    w_qkv, w_proj, w_fc, w_out = weights
    gains, offsets, attn_bias, out_bias, fc_bias = smalls
    hidden = layer_in.astype(f32)
    width = hidden.shape[-1]
    normed = layer_norm(hidden, gains[0], offsets[0]).astype(bf16)
    bias = jnp.concatenate([attn_bias[0], jnp.zeros((width,), f32), attn_bias[1]])
    project = (mm(normed, w_qkv) + bias).astype(bf16)
    mixed, log_total = attend_forward(project, length)
    after = hidden + mm(mixed, w_proj) + out_bias[0]
    normed_two = layer_norm(after, gains[1], offsets[1]).astype(bf16)
    inner = mm(normed_two, w_fc) + fc_bias
    active = gelu_tanh(inner).astype(bf16)
    result = (after + mm(active, w_out) + out_bias[1]).astype(bf16)
    return result, (layer_in, normed, project, mixed, log_total, after, normed_two, inner, active)


def row_sum(rows):
    return jnp.sum(rows.astype(f32), axis=0)


def layer_back(weights, smalls, kept, grad_out, length, send):
    w_qkv, w_proj, w_fc, w_out = weights
    gains, offsets, attn_bias, out_bias, fc_bias = smalls
    layer_in, normed, project, mixed, log_total, after, normed_two, inner, active = kept
    grad_w_out = send(mm_tn(active, grad_out).astype(bf16))
    grad_bias_two = row_sum(grad_out)
    grad_active = mm_nt(grad_out, w_out)
    _, gelu_pull = jax.vjp(gelu_tanh, inner)
    grad_inner = gelu_pull(grad_active)[0].astype(bf16)
    grad_w_fc = send(mm_tn(normed_two, grad_inner).astype(bf16))
    grad_fc_bias = row_sum(grad_inner)
    grad_normed_two = mm_nt(grad_inner, w_fc)
    _, norm_pull = jax.vjp(layer_norm, after, gains[1], offsets[1])
    grad_after, grad_gain_two, grad_offset_two = norm_pull(grad_normed_two)
    grad_after = grad_after + grad_out.astype(f32)
    grad_branch = grad_after.astype(bf16)
    grad_w_proj = send(mm_tn(mixed, grad_branch).astype(bf16))
    grad_bias_one = row_sum(grad_branch)
    grad_mixed = mm_nt(grad_branch, w_proj).astype(bf16)
    grad_q, grad_k, grad_v = attend_back(project, grad_mixed, mixed, log_total, length)
    grad_project = jnp.concatenate([grad_q, grad_k, grad_v], axis=-1)
    grad_w_qkv = send(mm_tn(normed, grad_project).astype(bf16))
    grad_normed = mm_nt(grad_project, w_qkv)
    _, first_pull = jax.vjp(layer_norm, layer_in.astype(f32), gains[0], offsets[0])
    grad_hidden, grad_gain_one, grad_offset_one = first_pull(grad_normed)
    grad_input = (grad_after + grad_hidden).astype(bf16)
    small = (
        jnp.stack(
            [
                grad_gain_one,
                grad_gain_two,
                grad_offset_one,
                grad_offset_two,
                row_sum(grad_q),
                row_sum(grad_v),
                grad_bias_one,
                grad_bias_two,
            ]
        ),
        grad_fc_bias,
    )
    return grad_input, (grad_w_qkv, grad_w_proj, grad_w_fc, grad_w_out), small


def swap(value):
    return lax.ppermute(value, "section", [(0, 1), (1, 0)])


def shards(
    block_input,
    positions,
    cotangent,
    w_qkv,
    w_proj,
    w_fc,
    w_out,
    ln_gain,
    ln_bias,
    attn_bias,
    out_bias,
    fc_bias,
):
    section = lax.axis_index("section")
    ctx_index = lax.axis_index("ctx")
    first = section == 0
    sections = lax.axis_size("section")
    ctxs = lax.axis_size("ctx")
    fsdps = lax.axis_size("fsdp")
    local_seqs, local_rows, width = block_input.shape
    length = positions.shape[1]
    per = -(-local_seqs // (sections * ctxs))
    slots = sections * ctxs * per
    spare = slots - local_seqs
    shard_width = ln_gain.shape[2]

    def trade(value):
        other = swap(value)
        return jnp.where(first, value, other), jnp.where(first, other, value)

    pack = jnp.concatenate(
        [ln_gain[0], ln_bias[0], attn_bias[0], out_bias[0], fc_bias[0].reshape(-1, shard_width)]
    )
    pack = lax.all_gather(pack, "fsdp", axis=0)
    packs = trade(pack)

    def unpack(packed):
        vectors = jnp.transpose(packed[:, :8], (1, 0, 2)).reshape(8, -1).astype(f32)
        fc = packed[:, 8:].reshape(-1).astype(f32)
        return vectors[0:2], vectors[2:4], vectors[4:6], vectors[6:8], fc

    smalls = [unpack(packed) for packed in packs]

    def halves(matrix):
        rows = matrix.shape[0] // 2
        low, high = matrix[:rows], matrix[rows:]
        arrived = swap(jnp.where(first, high, low))
        mine = jnp.where(first, low, high)
        return jnp.where(first, mine, arrived), jnp.where(first, arrived, mine)

    pieces = [halves(matrix[0]) for matrix in (w_qkv, w_proj, w_fc, w_out)]

    def whole_weight(piece):
        gathered = lax.all_gather(piece, "fsdp", axis=0)
        low, high = trade(gathered)
        return jnp.stack([low, high], axis=1).reshape(-1, piece.shape[-1])

    weights = [tuple(whole_weight(piece[layer]) for piece in pieces) for layer in range(2)]

    def own(padded):
        return lax.dynamic_slice_in_dim(padded, section * (ctxs * per), ctxs * per, 0)

    def bring(rows):
        padded = jnp.pad(rows, ((0, spare), (0, 0), (0, 0)))
        mine = own(padded).reshape(ctxs, per, local_rows, width)
        moved = lax.all_to_all(mine, "ctx", 0, 0, tiled=True)
        return jnp.transpose(moved, (1, 0, 2, 3)).reshape(per, length, width)

    places = own(jnp.pad(positions, ((0, spare), (0, 0)))).reshape(ctxs, per, length)
    places = lax.dynamic_index_in_dim(places, ctx_index, 0, keepdims=False)
    order = (
        lax.broadcasted_iota(jnp.int32, (per, length, length), 1) == places[:, None, :]
    ).astype(bf16)

    def to_sorted(rows):
        return (
            jnp.einsum("bpt,btd->bpd", order, rows, preferred_element_type=f32)
            .astype(bf16)
            .reshape(per * length, width)
        )

    def to_stored(rows):
        return jnp.einsum(
            "bpt,bpd->btd", order, rows.reshape(per, length, width), preferred_element_type=f32
        ).astype(bf16)

    def home(zero, one):
        arrived = swap(jnp.where(first, one, zero))
        mine = jnp.where(first, zero, one)
        both = jnp.stack([jnp.where(first, mine, arrived), jnp.where(first, arrived, mine)])
        both = both.reshape(sections, per, ctxs, local_rows, width)
        moved = lax.all_to_all(both, "ctx", 2, 2, tiled=True)
        ordered = jnp.transpose(moved, (0, 2, 1, 3, 4)).reshape(slots, local_rows, width)
        return ordered[:local_seqs][None]

    start = to_sorted(bring(block_input))
    grad_final = to_sorted(bring(cotangent))
    middle, kept_zero = layer_forward(weights[0], smalls[0], start, length)
    final, kept_one = layer_forward(weights[1], smalls[1], middle, length)
    section_out = home(to_stored(middle), to_stored(final))

    def send(grad):
        cut = grad.reshape(fsdps, 2, -1, grad.shape[-1])
        low, high = cut[:, 0], cut[:, 1]
        arrived = swap(jnp.where(first, high, low))
        mine = jnp.where(first, low, high)
        both = (mine.astype(f32) + arrived.astype(f32)).astype(bf16)
        scattered = lax.psum_scatter(both, "fsdp", scatter_dimension=0, tiled=False)
        return lax.psum(scattered, "ctx")

    grad_middle, grads_one, small_one = layer_back(
        weights[1], smalls[1], kept_one, grad_final, length, send
    )
    grad_start, grads_zero, small_zero = layer_back(
        weights[0], smalls[0], kept_zero, grad_middle, length, send
    )
    section_in_grad = home(to_stored(grad_start), to_stored(grad_middle))

    def finish(zero, one):
        arrived = swap(jnp.where(first, one, zero))
        mine = jnp.where(first, zero, one)
        low = jnp.where(first, mine, arrived)
        high = jnp.where(first, arrived, mine)
        return jnp.concatenate([low, high], axis=0).astype(f32)[None]

    big = [finish(zero, one) for zero, one in zip(grads_zero, grads_one)]

    def repack(small):
        vectors, fc = small
        vectors = jnp.transpose(vectors.reshape(8, fsdps, shard_width), (1, 0, 2))
        return jnp.concatenate([vectors, fc.reshape(fsdps, -1, shard_width)], axis=1)

    packed = jnp.stack([repack(small_zero), repack(small_one)])
    packed = lax.psum(packed, ("section", "ctx", "fsdp"))
    packed = lax.dynamic_index_in_dim(packed, section, 0, keepdims=False)
    packed = lax.dynamic_index_in_dim(packed, lax.axis_index("fsdp"), 0, keepdims=False)
    return (
        section_out,
        section_in_grad,
        *big,
        packed[None, 0:2],
        packed[None, 2:4],
        packed[None, 4:6],
        packed[None, 6:8],
        packed[8:].reshape(1, -1),
    )


def solution(mesh):
    matrix = P("section", "fsdp", None)
    vectors = P("section", None, "fsdp")
    rows_out = P("section", "fsdp", "ctx", None)
    return jax.shard_map(
        shards,
        mesh=mesh,
        in_specs=(
            P("fsdp", "ctx", None),
            P("fsdp", None),
            P("fsdp", "ctx", None),
            *([matrix] * 4),
            *([vectors] * 4),
            P("section", "fsdp"),
        ),
        out_specs=(
            rows_out,
            rows_out,
            *([matrix] * 4),
            *([vectors] * 4),
            P("section", "fsdp"),
        ),
        check_vma=False,
    )
```

```python
import functools

import jax
import jax.numpy as jnp
from jax import lax
from jax.experimental import pallas as pl
from jax.experimental.pallas import tpu as pltpu
from jax.sharding import PartitionSpec as P

H = 12
HD = 64
PAIR = 2 * HD
SCALE = HD**-0.5

masked_score = -1e30
norm_eps = 1e-05
f32 = jnp.float32
bf16 = jnp.bfloat16


def layer_norm(hidden, gain, offset):
    center = hidden - jnp.mean(hidden, axis=-1, keepdims=True)
    spread = jnp.mean(center * center, axis=-1, keepdims=True)
    return center * lax.rsqrt(spread + norm_eps) * gain + offset


def gelu_tanh(inputs):
    return jax.nn.gelu(inputs, approximate=True)


def mm(left, right):
    return lax.dot_general(left, right, (((1,), (0,)), ((), ())), preferred_element_type=f32)


def mm_nt(left, right):
    return lax.dot_general(left, right, (((1,), (1,)), ((), ())), preferred_element_type=f32)


def mm_tn(left, right):
    return lax.dot_general(left, right, (((0,), (0,)), ((), ())), preferred_element_type=f32)


def masked_scores(keys, queries, start, block):
    scores = mm_nt(keys, queries)
    down = lax.broadcasted_iota(jnp.int32, (block, block), 0)
    across = lax.broadcasted_iota(jnp.int32, (block, block), 1)
    corner = jnp.where(across >= down, scores[start:], masked_score)
    if start == 0:
        return corner
    return jnp.concatenate([scores[:start], corner], axis=0)


def attend_kernel(block, q_ref, k_ref, v_ref, o_ref, log_ref):
    length = q_ref.shape[0]
    for head in range(2):
        cols = slice(head * HD, (head + 1) * HD)
        for start in range(0, length, block):
            end = start + block
            queries = (q_ref[start:end, cols].astype(f32) * SCALE).astype(bf16)
            scores = masked_scores(k_ref[:end, cols], queries, start, block)
            top = jnp.max(scores, axis=0, keepdims=True)
            weights = jnp.exp(scores - top)
            total = jnp.sum(weights, axis=0, keepdims=True)
            mixed = mm_tn(v_ref[:end, cols], weights.astype(bf16)) / total
            o_ref[start:end, cols] = mixed.T.astype(bf16)
            log_ref[0, 0, head : head + 1, start:end] = top + jnp.log(total)


def attend_back_kernel(
    block, q_ref, k_ref, v_ref, do_ref, o_ref, log_ref, dq_ref, dk_ref, dv_ref, dk_sum, dv_sum
):
    length = q_ref.shape[0]
    for head in range(2):
        cols = slice(head * HD, (head + 1) * HD)
        for start in range(length - block, -1, -block):
            end = start + block
            queries = (q_ref[start:end, cols].astype(f32) * SCALE).astype(bf16)
            grads = do_ref[start:end, cols]
            product = grads.astype(f32) * o_ref[start:end, cols].astype(f32)
            delta = jnp.sum(product.T, axis=0, keepdims=True)
            keys = k_ref[:end, cols]
            scores = masked_scores(keys, queries, start, block)
            probs = jnp.exp(scores - log_ref[0, 0, head : head + 1, start:end])
            grad_probs = mm_nt(v_ref[:end, cols], grads)
            grad_scores = (probs * (grad_probs - delta)).astype(bf16)
            dv = mm(probs.astype(bf16), grads)
            dk = mm(grad_scores, queries)
            if end == length:
                dv_sum[:end, cols] = dv
                dk_sum[:end, cols] = dk
            else:
                dv_sum[:end, cols] += dv
                dk_sum[:end, cols] += dk
            dq = mm_tn(keys, grad_scores) * SCALE
            dq_ref[start:end, cols] = dq.T.astype(bf16)
    dk_ref[...] = dk_sum[...].astype(bf16)
    dv_ref[...] = dv_sum[...].astype(bf16)


def query_block(length):
    return 256 if length % 256 == 0 else length


def head_spec(length, offset):
    return pl.BlockSpec((length, PAIR), lambda b, h: (b, offset + h))


def log_spec(length):
    return pl.BlockSpec((1, 1, 2, length), lambda b, h: (b, h, 0, 0))


def attend_forward(project, length):
    rows = project.shape[0]
    count = rows // length
    pairs = H // 2
    return pl.pallas_call(
        functools.partial(attend_kernel, query_block(length)),
        grid=(count, pairs),
        in_specs=[head_spec(length, 0), head_spec(length, pairs), head_spec(length, 2 * pairs)],
        out_specs=[head_spec(length, 0), log_spec(length)],
        out_shape=[
            jax.ShapeDtypeStruct((rows, H * HD), bf16),
            jax.ShapeDtypeStruct((count, pairs, 2, length), f32),
        ],
        compiler_params=pltpu.CompilerParams(vmem_limit_bytes=40 * 1024 * 1024),
        cost_estimate=pl.CostEstimate(
            flops=8 * rows * length * H * HD,
            bytes_accessed=8 * rows * H * HD,
            transcendentals=rows * length * H // 2,
        ),
    )(project, project, project)


def attend_back(project, grad_mixed, mixed, log_total, length):
    rows = project.shape[0]
    count = rows // length
    pairs = H // 2
    return pl.pallas_call(
        functools.partial(attend_back_kernel, query_block(length)),
        grid=(count, pairs),
        in_specs=[
            head_spec(length, 0),
            head_spec(length, pairs),
            head_spec(length, 2 * pairs),
            head_spec(length, 0),
            head_spec(length, 0),
            log_spec(length),
        ],
        out_specs=[head_spec(length, 0)] * 3,
        out_shape=[jax.ShapeDtypeStruct((rows, H * HD), bf16)] * 3,
        scratch_shapes=[pltpu.VMEM((length, PAIR), f32)] * 2,
        compiler_params=pltpu.CompilerParams(vmem_limit_bytes=40 * 1024 * 1024),
        cost_estimate=pl.CostEstimate(
            flops=20 * rows * length * H * HD,
            bytes_accessed=16 * rows * H * HD,
            transcendentals=rows * length * H // 2,
        ),
    )(project, project, project, grad_mixed, mixed, log_total)


def layer_forward(weights, smalls, layer_in, length):
    w_qkv, w_proj, w_fc, w_out = weights
    gains, offsets, attn_bias, out_bias, fc_bias = smalls
    hidden = layer_in.astype(f32)
    width = hidden.shape[-1]
    normed = layer_norm(hidden, gains[0], offsets[0]).astype(bf16)
    bias = jnp.concatenate([attn_bias[0], jnp.zeros((width,), f32), attn_bias[1]])
    project = (mm(normed, w_qkv) + bias).astype(bf16)
    mixed, log_total = attend_forward(project, length)
    after = hidden + mm(mixed, w_proj) + out_bias[0]
    normed_two = layer_norm(after, gains[1], offsets[1]).astype(bf16)
    inner = mm(normed_two, w_fc) + fc_bias
    active = gelu_tanh(inner).astype(bf16)
    result = (after + mm(active, w_out) + out_bias[1]).astype(bf16)
    return result, (layer_in, normed, project, mixed, log_total, after, normed_two, inner, active)


def row_sum(rows):
    return jnp.sum(rows.astype(f32), axis=0)


def layer_back(weights, smalls, kept, grad_out, length, send):
    w_qkv, w_proj, w_fc, w_out = weights
    gains, offsets, attn_bias, out_bias, fc_bias = smalls
    layer_in, normed, project, mixed, log_total, after, normed_two, inner, active = kept
    grad_out, grad_w_out = lax.optimization_barrier(
        (grad_out, mm_tn(active, grad_out).astype(bf16))
    )
    grad_w_out = send(grad_w_out)
    grad_bias_two = row_sum(grad_out)
    grad_active = mm_nt(grad_out, w_out)
    _, gelu_pull = jax.vjp(gelu_tanh, inner)
    grad_inner = gelu_pull(grad_active)[0].astype(bf16)
    grad_inner, grad_w_fc = lax.optimization_barrier(
        (grad_inner, mm_tn(normed_two, grad_inner).astype(bf16))
    )
    grad_w_fc = send(grad_w_fc)
    grad_fc_bias = row_sum(grad_inner)
    grad_normed_two = mm_nt(grad_inner, w_fc)
    _, norm_pull = jax.vjp(layer_norm, after, gains[1], offsets[1])
    grad_after, grad_gain_two, grad_offset_two = norm_pull(grad_normed_two)
    grad_after = grad_after + grad_out.astype(f32)
    grad_branch = grad_after.astype(bf16)
    grad_branch, grad_w_proj = lax.optimization_barrier(
        (grad_branch, mm_tn(mixed, grad_branch).astype(bf16))
    )
    grad_w_proj = send(grad_w_proj)
    grad_bias_one = row_sum(grad_branch)
    grad_mixed = mm_nt(grad_branch, w_proj).astype(bf16)
    grad_q, grad_k, grad_v = attend_back(project, grad_mixed, mixed, log_total, length)
    grad_project = jnp.concatenate([grad_q, grad_k, grad_v], axis=-1)
    grad_project, grad_w_qkv = lax.optimization_barrier(
        (grad_project, mm_tn(normed, grad_project).astype(bf16))
    )
    grad_w_qkv = send(grad_w_qkv)
    grad_normed = mm_nt(grad_project, w_qkv)
    _, first_pull = jax.vjp(layer_norm, layer_in.astype(f32), gains[0], offsets[0])
    grad_hidden, grad_gain_one, grad_offset_one = first_pull(grad_normed)
    grad_input = (grad_after + grad_hidden).astype(bf16)
    small = (
        jnp.stack(
            [
                grad_gain_one,
                grad_gain_two,
                grad_offset_one,
                grad_offset_two,
                row_sum(grad_q),
                row_sum(grad_v),
                grad_bias_one,
                grad_bias_two,
            ]
        ),
        grad_fc_bias,
    )
    return grad_input, (grad_w_qkv, grad_w_proj, grad_w_fc, grad_w_out), small


def swap(value):
    return lax.ppermute(value, "section", [(0, 1), (1, 0)])


def cross(value, bit):
    return lax.ppermute(value, "fsdp", [(i, i ^ bit) for i in range(4)])


def add(left, right):
    return (left.astype(f32) + right.astype(f32)).astype(left.dtype)


def gather_fsdp(shard):
    if lax.axis_size("fsdp") != 4:
        return lax.all_gather(shard, "fsdp", axis=0)
    half = shard.shape[0] // 2
    near = cross(shard, 1)
    far = cross(shard, 2)
    corner = jnp.concatenate([cross(far[:half], 1), cross(near[half:], 2)], axis=0)
    index = lax.axis_index("fsdp")
    even, low = index % 2 == 0, index < 2
    a, b = jnp.where(even, shard, near), jnp.where(even, near, shard)
    c, d = jnp.where(even, far, corner), jnp.where(even, corner, far)
    return jnp.stack(
        [jnp.where(low, a, c), jnp.where(low, b, d), jnp.where(low, c, a), jnp.where(low, d, b)]
    )


def scatter_fsdp(parts):
    if lax.axis_size("fsdp") != 4:
        return lax.psum_scatter(parts, "fsdp", scatter_dimension=0, tiled=False)
    index = lax.axis_index("fsdp")
    half = parts.shape[1] // 2

    def part(bits):
        return lax.dynamic_index_in_dim(parts, index ^ bits, 0, keepdims=False)

    corner, far, near = part(3), part(2), part(1)
    from_near = cross(corner[:half], 1)
    from_far = cross(corner[half:], 2)
    far = jnp.concatenate([add(far[:half], from_near), far[half:]], axis=0)
    near = jnp.concatenate([near[:half], add(near[half:], from_far)], axis=0)
    total = part(0).astype(f32) + cross(near, 1).astype(f32) + cross(far, 2).astype(f32)
    return total.astype(parts.dtype)


def sum_ctx(value):
    if lax.axis_size("ctx") != 4:
        return lax.psum(value, "ctx")
    index = lax.axis_index("ctx")
    inner = (index == 1) | (index == 2)
    value = add(value, lax.ppermute(value, "ctx", [(0, 1), (3, 2)]))
    value = add(value, lax.ppermute(value, "ctx", [(1, 2), (2, 1)]))
    return jnp.where(inner, value, lax.ppermute(value, "ctx", [(1, 0), (2, 3)]))


def shards(
    block_input,
    positions,
    cotangent,
    w_qkv,
    w_proj,
    w_fc,
    w_out,
    ln_gain,
    ln_bias,
    attn_bias,
    out_bias,
    fc_bias,
):
    section = lax.axis_index("section")
    ctx_index = lax.axis_index("ctx")
    first = section == 0
    sections = lax.axis_size("section")
    ctxs = lax.axis_size("ctx")
    fsdps = lax.axis_size("fsdp")
    local_seqs, local_rows, width = block_input.shape
    length = positions.shape[1]
    per = -(-local_seqs // (sections * ctxs))
    slots = sections * ctxs * per
    spare = slots - local_seqs
    shard_width = ln_gain.shape[2]

    def trade(value):
        other = swap(value)
        return jnp.where(first, value, other), jnp.where(first, other, value)

    pack = jnp.concatenate(
        [ln_gain[0], ln_bias[0], attn_bias[0], out_bias[0], fc_bias[0].reshape(-1, shard_width)]
    )
    pack = gather_fsdp(pack)
    packs = trade(pack)

    def unpack(packed):
        vectors = jnp.transpose(packed[:, :8], (1, 0, 2)).reshape(8, -1).astype(f32)
        fc = packed[:, 8:].reshape(-1).astype(f32)
        return vectors[0:2], vectors[2:4], vectors[4:6], vectors[6:8], fc

    smalls = [unpack(packed) for packed in packs]

    def halves(matrix):
        rows = matrix.shape[0] // 2
        low, high = matrix[:rows], matrix[rows:]
        arrived = swap(jnp.where(first, high, low))
        mine = jnp.where(first, low, high)
        return jnp.where(first, mine, arrived), jnp.where(first, arrived, mine)

    pieces = [halves(matrix[0]) for matrix in (w_qkv, w_proj, w_fc, w_out)]

    def whole_weight(piece):
        low, high = trade(gather_fsdp(piece))
        return jnp.stack([low, high], axis=1).reshape(-1, piece.shape[-1])

    weights_zero = tuple(whole_weight(piece[0]) for piece in pieces)
    later = tuple(piece[1] for piece in pieces)
    w_qkv_zero, later = lax.optimization_barrier((weights_zero[0], later))
    weights_zero = (w_qkv_zero, *weights_zero[1:])
    weights = [weights_zero, tuple(whole_weight(piece) for piece in later)]

    def own(padded):
        return lax.dynamic_slice_in_dim(padded, section * (ctxs * per), ctxs * per, 0)

    def bring(rows):
        padded = jnp.pad(rows, ((0, spare), (0, 0), (0, 0)))
        mine = own(padded).reshape(ctxs, per, local_rows, width)
        moved = lax.all_to_all(mine, "ctx", 0, 0, tiled=True)
        return jnp.transpose(moved, (1, 0, 2, 3)).reshape(per, length, width)

    places = own(jnp.pad(positions, ((0, spare), (0, 0)))).reshape(ctxs, per, length)
    places = lax.dynamic_index_in_dim(places, ctx_index, 0, keepdims=False)
    order = (
        lax.broadcasted_iota(jnp.int32, (per, length, length), 1) == places[:, None, :]
    ).astype(bf16)
    order_back = (
        lax.broadcasted_iota(jnp.int32, (per, length, length), 2) == places[:, :, None]
    ).astype(bf16)

    def to_sorted(rows):
        return (
            jnp.einsum("bpt,btd->bpd", order, rows, preferred_element_type=f32)
            .astype(bf16)
            .reshape(per * length, width)
        )

    def spread(rows):
        stored = jnp.einsum(
            "btp,bpd->btd", order_back, rows.reshape(per, length, width), preferred_element_type=f32
        ).astype(bf16)
        cut = stored.reshape(per, ctxs, local_rows, width)
        moved = lax.all_to_all(cut, "ctx", 1, 1, tiled=True)
        return jnp.transpose(moved, (1, 0, 2, 3)).reshape(ctxs * per, local_rows, width)

    def home(zero, one):
        arrived = swap(jnp.where(first, one, zero))
        mine = jnp.where(first, zero, one)
        low, high = jnp.where(first, mine, arrived), jnp.where(first, arrived, mine)
        return jnp.concatenate([low, high], axis=0)[:local_seqs][None]

    start = to_sorted(bring(block_input))
    grad_final = to_sorted(bring(cotangent))
    middle, kept_zero = layer_forward(weights[0], smalls[0], start, length)
    final, kept_one = layer_forward(weights[1], smalls[1], middle, length)
    out_zero = spread(middle)
    out_one = spread(final)

    def send(grad):
        cut = grad.reshape(fsdps, 2, -1, grad.shape[-1])
        low, high = cut[:, 0], cut[:, 1]
        arrived = swap(jnp.where(first, high, low))
        mine = jnp.where(first, low, high)
        return sum_ctx(scatter_fsdp(add(mine, arrived)))

    grad_middle, grads_one, small_one = layer_back(
        weights[1], smalls[1], kept_one, grad_final, length, send
    )
    grad_middle, out_zero, out_one = lax.optimization_barrier((grad_middle, out_zero, out_one))
    in_one = spread(grad_middle)
    grad_start, grads_zero, small_zero = layer_back(
        weights[0], smalls[0], kept_zero, grad_middle, length, send
    )
    section_out = home(out_zero, out_one)
    section_in_grad = home(spread(grad_start), in_one)

    def finish(zero, one):
        arrived = swap(jnp.where(first, one, zero))
        mine = jnp.where(first, zero, one)
        low = jnp.where(first, mine, arrived)
        high = jnp.where(first, arrived, mine)
        return jnp.concatenate([low, high], axis=0).astype(f32)[None]

    big = [finish(zero, one) for zero, one in zip(grads_zero, grads_one)]

    def repack(small):
        vectors, fc = small
        vectors = jnp.transpose(vectors.reshape(8, fsdps, shard_width), (1, 0, 2))
        return jnp.concatenate([vectors, fc.reshape(fsdps, -1, shard_width)], axis=1)

    pack_zero, pack_one = repack(small_zero), repack(small_one)
    arrived = swap(jnp.where(first, pack_one, pack_zero))
    packed = sum_ctx(scatter_fsdp(jnp.where(first, pack_zero, pack_one) + arrived))
    return (
        section_out,
        section_in_grad,
        *big,
        packed[None, 0:2],
        packed[None, 2:4],
        packed[None, 4:6],
        packed[None, 6:8],
        packed[8:].reshape(1, -1),
    )


def solution(mesh):
    matrix = P("section", "fsdp", None)
    vectors = P("section", None, "fsdp")
    rows_out = P("section", "fsdp", "ctx", None)
    return jax.shard_map(
        shards,
        mesh=mesh,
        in_specs=(
            P("fsdp", "ctx", None),
            P("fsdp", None),
            P("fsdp", "ctx", None),
            *([matrix] * 4),
            *([vectors] * 4),
            P("section", "fsdp"),
        ),
        out_specs=(
            rows_out,
            rows_out,
            *([matrix] * 4),
            *([vectors] * 4),
            P("section", "fsdp"),
        ),
        check_vma=False,
    )
```
